32 devices in a mesh: clip: 2 (over y), tm: 8 (over z, x), tile: 2 (over core).
Axes of the slice: x: 2, y: 2, z: 4, core: 2. Of those that a mesh axis runs over, the one named last changes fastest.
Arguments:
- queries: bfloat16 [32, 256, 2048], P(('clip', 'tm'), 'tile'), parts along dimension 0, may hold values from -48 to 48
- keyvals: bfloat16 [2, 32, 256, 512], P(None, ('clip', 'tm'), 'tile'), parts along dimension 1, may hold values from -4 to 4
- proj_weight: bfloat16 [2048, 1024], P('tm', 'tile'), may hold values from -0.125 to 0.125
- norm_gain: float32 [1024], P('tile'), may hold values from 0.25 to 1.75
- frame_counts: int32 [32], P(('clip', 'tm')), parts along dimension 0, may hold values from 129 to 256, as said below
Outputs:
- dynamics: bfloat16 [32, 256, 1024], P(('clip', 'tm'), None, 'tile'), parts along dimension 0
The draws below stay inside these ranges and needn't reach their ends.
There are 2 independent parts, one for each index of `clip`. The reference program is written for one: setup_inputs(seed, part) draws one part's arguments, and reference() takes and returns one part's arrays. A program takes and returns all parts, laid end to end along the dimension named above; an argument that names none is the same for every part. Nothing has to cross between parts.
Inputs may be any that keep to these rules, and one draw needn't show every extreme that they name: `frame_counts`: every spatial tile of every frame holds a live slot; some frame is full.
All inputs are finite; a program needn't handle non-finite values.
Results may differ from the reference program's by a relative error of at most 0.013.
Values may be sent and summed in bfloat16 or wider, within the bound.
No kernel may reach another device: no remote copies, remote signals or barrier semaphores. Data moves between devices by JAX's collectives and lax.ppermute only.
A program may use at most 64 MiB of HBM per device.

```python
import jax
import jax.numpy as jnp
from jax import lax

FRAME_TOK = 256
QHEADS = 16
KVHEADS = 4
HEAD_DIM = 128
IDM_HEADS = 16
IDM_DIM = 64
WINDOW = 4
PARTNER = 16
QWIDTH = 2048
KVWIDTH = 512
LATENT = 1024
FRAMES = 16
TILES = 2
TILE_TOK = 128


def paired_inputs(key):
    folded = jax.random.fold_in(key, 101)
    query_key, value_key = jax.random.split(folded, 2)
    queries = jnp.clip(jax.random.normal(query_key, (FRAMES, FRAME_TOK, QWIDTH), jnp.float32), -4.0, 4.0)
    keyvals = jnp.clip(jax.random.normal(value_key, (2, FRAMES, FRAME_TOK, KVWIDTH), jnp.float32), -4.0, 4.0)
    return (queries, keyvals)


def draw_queries(key, part):
    return paired_inputs(key)[0].astype(jnp.bfloat16)


def draw_keyvals(key, part):
    return paired_inputs(key)[1].astype(jnp.bfloat16)


def draw_frame_counts(key, part):
    folded = jax.random.fold_in(key, 202)
    count_key, pick_key = jax.random.split(folded)
    lowest = FRAME_TOK - TILE_TOK + 1
    counts = jax.random.randint(count_key, (FRAMES,), lowest, FRAME_TOK + 1)
    picked = jax.random.permutation(pick_key, FRAMES)
    counts = counts.at[picked[0]].set(FRAME_TOK).at[picked[1]].set(lowest)
    return counts.astype(jnp.int32)


def level_of(stream_key, shape, cuts, low, high):
    def one(axis_at, parts):
        steps = jax.random.uniform(jax.random.fold_in(jax.random.fold_in(stream_key, 6), axis_at), (parts,), jnp.float32, low / len(cuts), high / len(cuts))
        return jnp.repeat(jnp.exp(steps), shape[axis_at] // parts).reshape((-1,) + (1,) * (len(shape) - axis_at - 1))

    loudness = one(*cuts[0])
    for cut in cuts[1:]:
        loudness = loudness * one(*cut)
    return loudness


def noise(own_key, shape, deviation, limit, pieces=(), kind=jnp.bfloat16):
    values = deviation * jax.random.normal(own_key, shape, jnp.float32)
    if pieces:
        values = values * level_of(own_key, shape, pieces, -0.22, 0.18)
    return jnp.clip(values, -limit, limit).astype(kind)


def setup_inputs(seed: int = 0, part: int = 0) -> dict:
    arg_keys = jax.random.split(jax.random.key(seed), 6)
    own_keys = jax.random.split(jax.random.fold_in(arg_keys[5], part), 6)
    return {
        "queries": draw_queries(jax.random.fold_in(jax.random.fold_in(arg_keys[5], part), 71), part),
        "keyvals": draw_keyvals(jax.random.fold_in(jax.random.fold_in(arg_keys[5], part), 71), part),
        "proj_weight": noise(arg_keys[2], (QWIDTH, LATENT), QWIDTH ** -0.5, 0.125, ((0, 8), (1, 2))),
        "norm_gain": jnp.clip(1.0 + 0.15 * jax.random.normal(arg_keys[3], (LATENT,), jnp.float32), 0.25, 1.75),
        "frame_counts": draw_frame_counts(jax.random.fold_in(jax.random.fold_in(arg_keys[5], part), 71), part),
    }


def window_attention(query_block, key_block, value_block, live_keys):
    row_count = query_block.shape[0]
    grouped = query_block.astype(jnp.float32).reshape(row_count, KVHEADS, QHEADS // KVHEADS, HEAD_DIM)
    scores = jnp.einsum('ikgd,jkd->ikgj', grouped, key_block.astype(jnp.float32)) * HEAD_DIM ** (-0.5)
    key_mask = live_keys[None, None, None, :]
    row_max = lax.optimization_barrier(jnp.max(jnp.where(key_mask, scores, -1e+30), axis=-1, keepdims=True))
    weights = jnp.where(key_mask, jnp.exp(jnp.where(key_mask, scores, row_max) - row_max), 0.0)
    normalized = (weights / lax.optimization_barrier(jnp.sum(weights, axis=-1, keepdims=True))).astype(jnp.bfloat16)
    blended = jnp.einsum('ikgj,jkd->ikgd', normalized.astype(jnp.float32), value_block.astype(jnp.float32))
    return blended.astype(jnp.bfloat16).reshape(row_count, QWIDTH)

def normalize_heads(latent_block, gain):
    width = latent_block.shape[-1]
    heads = width // IDM_DIM
    values = latent_block.astype(jnp.float32).reshape(latent_block.shape[:-1] + (heads, IDM_DIM))
    scaled = values * lax.rsqrt(lax.optimization_barrier(jnp.mean(values * values, axis=-1, keepdims=True)) + 1e-06)
    scaled = scaled * gain.astype(jnp.float32).reshape(heads, IDM_DIM)
    return scaled.astype(jnp.bfloat16).reshape(latent_block.shape)

def reference(queries, keyvals, proj_weight, norm_gain, frame_counts):
    tile_tokens = FRAME_TOK // TILES
    lead_frames = WINDOW - 1
    padded_kv = jnp.concatenate([jnp.zeros((2, lead_frames, FRAME_TOK, KVWIDTH), keyvals.dtype), keyvals], axis=1)
    padded_counts = jnp.concatenate([jnp.zeros((lead_frames,), jnp.int32), frame_counts.astype(jnp.int32)])
    slot_index = jnp.arange(FRAME_TOK, dtype=jnp.int32).reshape(TILES, tile_tokens)

    def first_section(frame_index):
        query_frame = lax.dynamic_index_in_dim(queries, frame_index, 0, keepdims=False).reshape(TILES, tile_tokens, QWIDTH)
        window_kv = lax.dynamic_slice_in_dim(padded_kv, frame_index, WINDOW, 1)
        window_counts = lax.dynamic_slice_in_dim(padded_counts, frame_index, WINDOW, 0)
        tiled_kv = window_kv.reshape(2, WINDOW, TILES, tile_tokens, KVHEADS, HEAD_DIM)
        tiled_kv = tiled_kv.transpose(0, 2, 1, 3, 4, 5).reshape(2, TILES, WINDOW * tile_tokens, KVHEADS, HEAD_DIM)
        live_keys = slot_index[None, :, :] < window_counts[:, None, None]
        live_keys = live_keys.transpose(1, 0, 2).reshape(TILES, WINDOW * tile_tokens)
        result = jax.vmap(window_attention)(query_frame, tiled_kv[0], tiled_kv[1], live_keys)
        return result.reshape(FRAME_TOK, QWIDTH)
    attended = lax.map(first_section, jnp.arange(FRAMES, dtype=jnp.int32))
    latent = jnp.dot(attended.reshape(FRAMES * FRAME_TOK, QWIDTH), proj_weight, preferred_element_type=jnp.float32)
    latent = latent.astype(jnp.bfloat16).reshape(FRAMES, FRAME_TOK, LATENT)
    normed = normalize_heads(latent, norm_gain)
    blank_frames = jnp.zeros((PARTNER, FRAME_TOK, LATENT), jnp.bfloat16)
    padded_normed = jnp.concatenate([blank_frames, normed, blank_frames], axis=0)
    blank_counts = jnp.zeros((PARTNER,), jnp.int32)
    padded_live = jnp.concatenate([blank_counts, frame_counts.astype(jnp.int32), blank_counts])
    slot_all = jnp.arange(FRAME_TOK, dtype=jnp.int32)

    def second_section(frame_index):
        key_frames = []
        live_parts = []
        for offset_frames in (0, PARTNER, 2 * PARTNER):
            key_frames.append(lax.dynamic_index_in_dim(padded_normed, frame_index + offset_frames, 0, keepdims=False))
            count_here = lax.dynamic_index_in_dim(padded_live, frame_index + offset_frames, 0, keepdims=False)
            live_parts.append(slot_all < count_here)
        key_rows = jnp.concatenate(key_frames, axis=0).reshape(3 * FRAME_TOK, IDM_HEADS, IDM_DIM).astype(jnp.float32)
        live_keys = jnp.concatenate(live_parts)
        query_rows = key_frames[1].reshape(FRAME_TOK, IDM_HEADS, IDM_DIM).astype(jnp.float32)
        scores = jnp.einsum('ihd,jhd->ihj', query_rows, key_rows) * IDM_DIM ** (-0.5)
        weights = jnp.where(live_keys[None, None, :], jnp.exp(scores), 0.0)
        normalized = (weights / lax.optimization_barrier(jnp.sum(weights, axis=-1, keepdims=True))).astype(jnp.bfloat16)
        blended = jnp.einsum('ihj,jhd->ihd', normalized.astype(jnp.float32), key_rows)
        return blended.astype(jnp.bfloat16).reshape(FRAME_TOK, LATENT)
    return lax.map(second_section, jnp.arange(FRAMES, dtype=jnp.int32))
```

```python
import functools
import math

import jax
import jax.numpy as jnp
from jax import lax
from jax.experimental import pallas as pl
from jax.experimental.pallas import tpu as pltpu
from jax.sharding import PartitionSpec as P

QHEADS = 16
KVHEADS = 4
HEAD_DIM = 128
IDM_DIM = 64
WINDOW = 4
PARTNER = 16
LOG2E = math.log2(math.e)
COUNT_ROWS = 16
BF16 = jnp.bfloat16
F32 = jnp.float32


def passed_along(value, axis, steps):
    count = lax.axis_size(axis)
    initial, last = (max(0, -steps), min(count, count - steps))
    return lax.ppermute(value, axis, [(source, source + steps) for source in range(initial, last)])


def swapped(value, axis, mask):
    count = lax.axis_size(axis)
    return lax.ppermute(value, axis, [(source, source ^ mask) for source in range(count)])


def dot(left, right):
    return lax.dot_general(left, right, (((1,), (0,)), ((), ())), preferred_element_type=F32)


def dot_t(left, right):
    return lax.dot_general(left, right, (((1,), (1,)), ((), ())), preferred_element_type=F32)


VMEM_SPEC = pl.BlockSpec(memory_space=pltpu.VMEM)
SMEM_SPEC = pl.BlockSpec(memory_space=pltpu.SMEM)


def prepare_kernel(counts_ref, half_ref, kv_ref, weight_ref, *outs):
    frames, tokens = kv_ref.shape[1:3]
    for frame in range(frames):
        out = outs[frame]
        for which in range(2):
            out[which, :tokens, :] = kv_ref[which, frame]
            out[which, tokens:, :] = jnp.full(
                (COUNT_ROWS, kv_ref.shape[3]), counts_ref[frame].astype(F32)
            ).astype(BF16)
    columns = outs[frames].shape[1]
    start = pl.multiple_of(half_ref[0] * columns, columns)
    outs[frames][...] = weight_ref[:, pl.ds(start, columns)]


def prepare(counts, half, keyvals, weight, columns):
    frames, tokens, width = keyvals.shape[1:]
    payload = jax.ShapeDtypeStruct((2, tokens + COUNT_ROWS, width), BF16)
    return pl.pallas_call(
        prepare_kernel,
        out_shape=[payload] * frames + [jax.ShapeDtypeStruct((weight.shape[0], columns), BF16)],
        in_specs=[SMEM_SPEC, SMEM_SPEC, VMEM_SPEC, VMEM_SPEC],
        out_specs=[VMEM_SPEC] * (frames + 1),
        name="prepare",
        cost_estimate=pl.CostEstimate(flops=0, bytes_accessed=2 << 20, transcendentals=0),
    )(counts, half, keyvals, weight)


def window_kernel(counts_ref, tile_ref, query_ref, own_ref, *rest):
    lead_refs, out_ref = rest[:-1], rest[-1]
    frames, tokens, columns = query_ref.shape
    groups = columns // HEAD_DIM
    slot = tile_ref[0] * tokens + lax.broadcasted_iota(jnp.int32, (1, tokens), 1)
    keys, values, biases = [], [], []
    ones = jnp.ones((tokens, HEAD_DIM), BF16)
    for ref in lead_refs:
        keys.append(ref[0, :tokens, :])
        values.append(jnp.concatenate([ref[1, :tokens, :], ones], axis=1))
        live = slot.astype(F32) < ref[0, tokens : tokens + COUNT_ROWS, :].astype(F32)[0:1, :tokens]
        biases.append(jnp.where(live, 0.0, -1e30))
    for frame in range(frames):
        keys.append(own_ref[0, frame])
        values.append(jnp.concatenate([own_ref[1, frame], ones], axis=1))
        biases.append(jnp.where(slot < counts_ref[frame], 0.0, -1e30))
    factor = HEAD_DIM ** (-0.5) * LOG2E
    for frame in range(frames):
        window = slice(frame, frame + WINDOW)
        key_block = jnp.concatenate(keys[window], axis=0)
        value_block = jnp.concatenate(values[window], axis=0)
        bias = jnp.concatenate(biases[window], axis=1)
        for group in range(groups):
            lanes = slice(group * HEAD_DIM, (group + 1) * HEAD_DIM)
            scores = dot_t(query_ref[frame, :, lanes], key_block) + bias
            row_max = jnp.max(scores, axis=1, keepdims=True)
            weights = jnp.exp2((scores - row_max) * factor).astype(BF16)
            both = dot(weights, value_block)
            out_ref[frame, :, lanes] = (both[:, :HEAD_DIM] / both[:, HEAD_DIM:]).astype(BF16)


def window_attention(counts, tile, queries, keyvals, leads):
    frames, tokens, width = queries.shape
    groups = QHEADS // KVHEADS
    lead_spec = pl.BlockSpec((2, tokens + COUNT_ROWS, HEAD_DIM), lambda head: (0, 0, head))
    query_spec = pl.BlockSpec((frames, tokens, groups * HEAD_DIM), lambda head: (0, 0, head))
    flops = 4 * frames * tokens * WINDOW * tokens * width
    return pl.pallas_call(
        window_kernel,
        grid=(KVHEADS,),
        out_shape=jax.ShapeDtypeStruct(queries.shape, BF16),
        in_specs=[
            SMEM_SPEC,
            SMEM_SPEC,
            query_spec,
            pl.BlockSpec((2, frames, tokens, HEAD_DIM), lambda head: (0, 0, 0, head)),
        ]
        + [lead_spec] * len(leads),
        out_specs=query_spec,
        name="window",
        cost_estimate=pl.CostEstimate(flops=flops, bytes_accessed=4 << 20, transcendentals=0),
    )(counts, tile, queries, keyvals, *leads)


def idm_kernel(counts_ref, place_ref, own_ref, other_ref, gain_ref, *rest):
    pieces = place_ref.shape[0] - 2
    weight_refs, out_ref = rest[:pieces], rest[-1]
    frames, tokens = own_ref.shape[:2]
    depth, columns = weight_refs[0].shape
    tile = place_ref[1]
    total = None
    for piece in range(pieces):
        rows = pl.ds(pl.multiple_of(place_ref[2 + piece] * depth, depth), depth)
        left = jnp.concatenate(
            [ref[frame, :, rows] for frame in range(frames) for ref in (own_ref, other_ref)], axis=0
        )
        term = dot(left, weight_refs[piece][...])
        total = term if total is None else total + term
    latent = total.astype(BF16).astype(F32)
    square = latent * latent
    high = square.astype(BF16)
    low = (square - high.astype(F32)).astype(BF16)
    same_head = (
        lax.broadcasted_iota(jnp.int32, (columns, columns), 0) // IDM_DIM
        == lax.broadcasted_iota(jnp.int32, (columns, columns), 1) // IDM_DIM
    )
    adder = jnp.where(same_head, 1.0, 0.0).astype(BF16)
    mean = (dot(high, adder) + dot(low, adder)) * (1.0 / IDM_DIM)
    normed = (latent * lax.rsqrt(mean + 1e-06) * gain_ref[...]).astype(BF16)
    frame_tokens = 2 * tokens
    width = 2 * IDM_DIM
    factor = IDM_DIM ** (-0.5) * LOG2E
    row = lax.broadcasted_iota(jnp.int32, (frame_tokens, width), 0)
    lane = lax.broadcasted_iota(jnp.int32, (frame_tokens, width), 1)
    slot = jnp.where(row < tokens, row + tile * tokens, row - tile * tokens)
    zero = jnp.zeros((frame_tokens, width), BF16)
    heads = [lane < IDM_DIM, lane >= IDM_DIM]
    places = [
        pl.ds(pl.multiple_of(tile * tokens, tokens), tokens),
        pl.ds(pl.multiple_of((1 - tile) * tokens, tokens), tokens),
    ]
    for frame in range(frames):
        live = slot < counts_ref[frame]
        for pair in range(columns // width):
            lanes = slice(pair * width, (pair + 1) * width)
            rows = normed[frame * frame_tokens : (frame + 1) * frame_tokens, lanes]
            asked = jnp.concatenate([jnp.where(head, rows, zero) for head in heads], axis=0)
            weights = jnp.exp2(dot_t(asked, rows) * factor).astype(BF16)
            answers = jnp.concatenate(
                [
                    jnp.concatenate(
                        [
                            jnp.where(head & live, rows, zero),
                            jnp.where(head & live, 1.0, 0.0).astype(BF16),
                        ],
                        axis=1,
                    )
                    for head in heads
                ],
                axis=0,
            )
            both = dot(
                jnp.concatenate([weights[:frame_tokens], weights[frame_tokens:]], axis=1), answers
            )
            blended = (both[:, :width] / both[:, width:]).astype(BF16)
            out_ref[frame, places[0], lanes] = blended[:tokens]
            out_ref[frame, places[1], lanes] = blended[tokens:]


def idm_half(counts, place, own, other, gain, weights, own_weight, previous):
    frames, tokens, width = own.shape
    columns = weights[-1].shape[1]
    depth = weights[-1].shape[0]
    half_block = lambda step, counts_ref, place_ref: (0, place_ref[0])
    full = lambda shape: pl.BlockSpec(shape, lambda step, *refs: (0,) * len(shape))
    operands = [own, other, gain]
    specs = [full(own.shape), full(other.shape), pl.BlockSpec((1, columns), half_block)]
    if own_weight is not None:
        operands.append(own_weight)
        specs.append(pl.BlockSpec((depth, columns), half_block))
    operands += weights
    specs += [full((depth, columns))] * len(weights)
    aliases = {}
    if previous is not None:
        aliases = {2 + len(operands): 0}
        operands.append(previous)
        specs.append(pl.BlockSpec(memory_space=pl.ANY))
    flops = 4 * frames * tokens * width * columns
    return pl.pallas_call(
        idm_kernel,
        grid_spec=pltpu.PrefetchScalarGridSpec(
            num_scalar_prefetch=2,
            grid=(1,),
            in_specs=specs,
            out_specs=pl.BlockSpec(
                (frames, 2 * tokens, columns),
                lambda step, counts_ref, place_ref: (0, 0, place_ref[0]),
            ),
        ),
        out_shape=jax.ShapeDtypeStruct((frames, 2 * tokens, gain.shape[1]), BF16),
        input_output_aliases=aliases,
        name="idm",
        cost_estimate=pl.CostEstimate(flops=flops, bytes_accessed=4 << 20, transcendentals=0),
    )(counts, place, *operands)


def planned(queries, keyvals, proj_weight, norm_gain, frame_counts):
    clip = lax.axis_index("clip")
    place = lax.axis_index("tm")
    tile = lax.axis_index("tile")
    columns = proj_weight.shape[1] // 2
    half = clip.reshape(1)
    first, second, mine = prepare(frame_counts, half, keyvals, proj_weight, columns)
    side = place % 2
    near = swapped(mine, "tm", 2)
    lead_3 = passed_along(second, "tm", 2)
    beside = swapped(mine, "tm", 1)
    lead_2 = passed_along(first, "tm", 1)
    far = [swapped(mine, "tm", 4), swapped(mine, "tm", 6)]
    lead_1 = swapped(jnp.where(side == 1, lead_3, second), "tm", 1)
    leads = (lead_3, lead_2, lead_1)
    near_side = swapped(near, "tm", 1)
    across_1 = swapped(jnp.concatenate([near, beside], axis=0), "clip", 1)
    far_both = jnp.concatenate(far, axis=0)
    far_side = swapped(far_both, "tm", 1)
    across_2 = swapped(far_both, "clip", 1)
    across_3 = swapped(jnp.concatenate([near_side, far_side], axis=0), "clip", 1)
    own = window_attention(frame_counts, tile.reshape(1), queries, keyvals, leads)
    other = swapped(own, "tile", 1)
    depth = mine.shape[0]
    cut = lambda array: [array[i : i + depth] for i in range(0, array.shape[0], depth)]
    gain = norm_gain.reshape(1, -1)
    order_1 = [0, 2, 1, 4, 6, 3, 5, 7]
    order_2 = [0, 2, 1, 4, 6, 3, 5, 7]
    table = lambda which, order: jnp.stack(
        [which, tile] + [place ^ step for step in order]
    ).astype(jnp.int32)
    out = idm_half(
        frame_counts, table(clip, order_1), own, other, gain,
        [mine, near, beside] + far + [near_side] + cut(far_side), None, None,
    )
    return idm_half(
        frame_counts, table(1 - clip, order_2), own, other, gain,
        cut(across_1) + cut(across_2) + cut(across_3), proj_weight, out,
    )


def general(queries, keyvals, proj_weight, norm_gain, frame_counts):
    frames_here, tile_tokens = queries.shape[:2]
    tile = lax.axis_index("tile")
    columns = proj_weight.shape[1]
    half = jnp.zeros((1,), jnp.int32)
    pieces = prepare(frame_counts, half, keyvals, proj_weight, columns)
    leads = []
    for back in range(WINDOW - 1, 0, -1):
        hops = -(-back // frames_here)
        leads.append(passed_along(pieces[hops * frames_here - back], "tm", hops))
    own = window_attention(frame_counts, tile.reshape(1), queries, keyvals, leads)
    weight = lax.all_gather(proj_weight, "tm", axis=0, tiled=True)
    both = lax.all_gather(own, "tile", axis=1, tiled=True)
    summed = jnp.dot(
        both.reshape(-1, both.shape[2]), weight, preferred_element_type=F32
    )
    latent = summed.astype(BF16).reshape(frames_here, 2 * tile_tokens, columns)
    normed = normalize_heads(latent, norm_gain)
    return partner_attention(normed, frame_counts)


def normalize_heads(latent_block, gain):
    width = latent_block.shape[-1]
    heads = width // IDM_DIM
    values = latent_block.astype(F32).reshape(latent_block.shape[:-1] + (heads, IDM_DIM))
    scaled = values * lax.rsqrt(jnp.mean(values * values, axis=-1, keepdims=True) + 1e-06)
    scaled = scaled * gain.reshape(heads, IDM_DIM)
    return scaled.astype(BF16).reshape(latent_block.shape)


def partner_attention(normed, frame_counts):
    frames_here, frame_tokens, width = normed.shape
    heads_here = width // IDM_DIM
    distance = PARTNER // frames_here
    before_normed, before_counts = passed_along((normed, frame_counts), "tm", distance)
    after_normed, after_counts = passed_along((normed, frame_counts), "tm", -distance)
    slot_all = jnp.arange(frame_tokens, dtype=jnp.int32)
    results = []
    for frame_index in range(frames_here):
        key_rows = jnp.concatenate(
            [before_normed[frame_index], normed[frame_index], after_normed[frame_index]], axis=0
        )
        key_rows = key_rows.reshape(3 * frame_tokens, heads_here, IDM_DIM)
        live_keys = jnp.concatenate(
            [
                slot_all < before_counts[frame_index],
                slot_all < frame_counts[frame_index],
                slot_all < after_counts[frame_index],
            ]
        )
        query_rows = normed[frame_index].reshape(frame_tokens, heads_here, IDM_DIM)
        scores = jnp.einsum(
            "ihd,jhd->ihj", query_rows, key_rows, preferred_element_type=F32
        ) * IDM_DIM ** (-0.5)
        weights = jnp.where(live_keys[None, None, :], jnp.exp(scores), 0.0)
        normalized = (weights / jnp.sum(weights, axis=-1, keepdims=True)).astype(BF16)
        blended = jnp.einsum("ihj,jhd->ihd", normalized, key_rows, preferred_element_type=F32)
        results.append(blended.astype(BF16).reshape(frame_tokens, width))
    return jnp.stack(results)


def solution(mesh):
    sizes = mesh.shape

    def local(queries, keyvals, proj_weight, norm_gain, frame_counts):
        frames_here = queries.shape[0]
        no_partner = PARTNER >= frames_here * sizes["tm"]
        eight_by_two = sizes["tm"] == 8 and sizes["clip"] == 2 and sizes["tile"] == 2
        if eight_by_two and no_partner and frames_here == 2:
            chosen = planned
        else:
            chosen = general
        return chosen(queries, keyvals, proj_weight, norm_gain, frame_counts)

    in_specs = (
        P(("clip", "tm"), "tile", None),
        P(None, ("clip", "tm"), "tile", None),
        P("tm", "tile"),
        P("tile"),
        P(("clip", "tm")),
    )
    out_specs = P(("clip", "tm"), None, "tile")
    return jax.shard_map(local, mesh=mesh, in_specs=in_specs, out_specs=out_specs, check_vma=False)
```

```python
import functools
import math

import jax
import jax.numpy as jnp
from jax import lax
from jax.experimental import pallas as pl
from jax.experimental.pallas import tpu as pltpu
from jax.sharding import PartitionSpec as P


QHEADS = 16
KVHEADS = 4
HEAD_DIM = 128
IDM_DIM = 64
WINDOW = 4
PARTNER = 16
LOG2E = math.log2(math.e)
COUNT_ROWS = 16
BF16 = jnp.bfloat16
F32 = jnp.float32


def passed_along(value, axis, steps):
    count = lax.axis_size(axis)
    initial, last = (max(0, -steps), min(count, count - steps))
    return lax.ppermute(value, axis, [(source, source + steps) for source in range(initial, last)])


def swapped(value, axis, mask):
    count = lax.axis_size(axis)
    return lax.ppermute(value, axis, [(source, source ^ mask) for source in range(count)])


def dot(left, right):
    return lax.dot_general(left, right, (((1,), (0,)), ((), ())), preferred_element_type=F32)


def dot_t(left, right):
    return lax.dot_general(left, right, (((1,), (1,)), ((), ())), preferred_element_type=F32)


VMEM_SPEC = pl.BlockSpec(memory_space=pltpu.VMEM)
SMEM_SPEC = pl.BlockSpec(memory_space=pltpu.SMEM)
HBM_SPEC = pl.BlockSpec(memory_space=pl.ANY)


def params(mib):
    return pltpu.CompilerParams(vmem_limit_bytes=mib << 20)


def prepare_kernel(split, counts_ref, kv_ref, weight_ref, *outs):
    frames, tokens = kv_ref.shape[1:3]
    if split:
        columns = outs[frames].shape[1]
        start = pl.multiple_of(lax.axis_index("clip") * columns, columns)
        outs[frames][...] = weight_ref[:, pl.ds(start, columns)]
    for frame in range(frames):
        out = outs[frame]
        for which in range(2):
            out[which, :tokens, :] = kv_ref[which, frame]
            out[which, tokens:, :] = jnp.full(
                (COUNT_ROWS, kv_ref.shape[3]), counts_ref[frame].astype(F32)
            ).astype(BF16)


def prepare(counts, keyvals, weight, split):
    frames, tokens, width = keyvals.shape[1:]
    shapes = [jax.ShapeDtypeStruct((2, tokens + COUNT_ROWS, width), BF16)] * frames
    if split:
        shapes.append(jax.ShapeDtypeStruct((weight.shape[0], weight.shape[1] // 2), BF16))
    return pl.pallas_call(
        functools.partial(prepare_kernel, split),
        out_shape=shapes,
        in_specs=[SMEM_SPEC, VMEM_SPEC, VMEM_SPEC],
        out_specs=[VMEM_SPEC] * len(shapes),
        name="prepare",
        compiler_params=params(4),
        cost_estimate=pl.CostEstimate(flops=0, bytes_accessed=2 << 20, transcendentals=0),
    )(counts, keyvals, weight)


def window_kernel(counts_ref, query_ref, own_ref, *rest):
    lead_refs, out_ref = rest[:-1], rest[-1]
    frames, tokens, width = query_ref.shape
    groups = QHEADS // KVHEADS
    slot = lax.axis_index("tile") * tokens + lax.broadcasted_iota(jnp.int32, (1, tokens), 1)
    biases = []
    for ref in lead_refs:
        count = ref[0, tokens : tokens + COUNT_ROWS, 0:tokens].astype(F32)[0:1, :]
        biases.append(jnp.where(slot.astype(F32) < count, 0.0, -1e30))
    for frame in range(frames):
        biases.append(jnp.where(slot < counts_ref[frame], 0.0, -1e30))
    ones = jnp.ones((WINDOW * tokens, HEAD_DIM), BF16)
    factor = HEAD_DIM ** (-0.5) * LOG2E
    for head in range(width // HEAD_DIM // groups):
        here = slice(head * HEAD_DIM, (head + 1) * HEAD_DIM)
        keys = [ref[0, :tokens, here] for ref in lead_refs]
        values = [ref[1, :tokens, here] for ref in lead_refs]
        keys += [own_ref[0, frame, :, here] for frame in range(frames)]
        values += [own_ref[1, frame, :, here] for frame in range(frames)]
        for frame in range(frames):
            window = slice(frame, frame + WINDOW)
            key_block = jnp.concatenate(keys[window], axis=0)
            value_block = jnp.concatenate([jnp.concatenate(values[window], axis=0), ones], axis=1)
            bias = jnp.concatenate(biases[window], axis=1)
            lanes = [
                slice((head * groups + group) * HEAD_DIM, (head * groups + group + 1) * HEAD_DIM)
                for group in range(groups)
            ]
            asked = jnp.concatenate([query_ref[frame, :, lane] for lane in lanes], axis=0)
            scores = dot_t(asked, key_block) + bias
            row_max = jnp.max(scores, axis=1, keepdims=True)
            weights = jnp.exp2((scores - row_max) * factor).astype(BF16)
            both = dot(weights, value_block)
            blended = (both[:, :HEAD_DIM] / both[:, HEAD_DIM:]).astype(BF16)
            for group in range(groups):
                out_ref[frame, :, lanes[group]] = blended[group * tokens : (group + 1) * tokens]


def window_attention(counts, queries, keyvals, leads):
    frames, tokens, width = queries.shape
    flops = 4 * frames * tokens * WINDOW * tokens * width
    return pl.pallas_call(
        window_kernel,
        out_shape=jax.ShapeDtypeStruct(queries.shape, BF16),
        in_specs=[SMEM_SPEC] + [VMEM_SPEC] * (2 + len(leads)),
        out_specs=VMEM_SPEC,
        name="window",
        compiler_params=params(16),
        cost_estimate=pl.CostEstimate(flops=flops, bytes_accessed=4 << 20, transcendentals=0),
    )(counts, queries, keyvals, *leads)


def idm_rows(tile, half, steps, counts_ref, own_ref, other_ref, gain_ref, weight_refs, store):
    frames, tokens = own_ref.shape[:2]
    place = lax.axis_index("tm")
    columns = weight_refs[0].shape[1]
    depth = own_ref.shape[2] // len(steps)
    wide = pl.ds(pl.multiple_of(half * columns, columns), columns)
    total = None
    at = 0
    for ref in weight_refs:
        for start in range(0, ref.shape[0], depth):
            block = place ^ steps[at]
            at += 1
            rows = pl.ds(pl.multiple_of(block * depth, depth), depth)
            left = jnp.concatenate(
                [part[frame, :, rows] for frame in range(frames) for part in (own_ref, other_ref)],
                axis=0,
            )
            if ref.shape[1] == columns:
                right = ref[start : start + depth, :]
            else:
                right = ref[start : start + depth, wide]
            term = dot(left, right)
            total = term if total is None else total + term
    latent = total.astype(BF16).astype(F32)
    square = latent * latent
    high = square.astype(BF16)
    low = (square - high.astype(F32)).astype(BF16)
    same_head = (
        lax.broadcasted_iota(jnp.int32, (columns, columns), 0) // IDM_DIM
        == lax.broadcasted_iota(jnp.int32, (columns, columns), 1) // IDM_DIM
    )
    adder = jnp.where(same_head, 1.0, 0.0).astype(BF16)
    mean = (dot(high, adder) + dot(low, adder)) * (1.0 / IDM_DIM)
    normed = (latent * lax.rsqrt(mean + 1e-06) * gain_ref[:, wide]).astype(BF16)
    frame_tokens = 2 * tokens
    width = 2 * IDM_DIM
    factor = IDM_DIM ** (-0.5) * LOG2E
    row = lax.broadcasted_iota(jnp.int32, (frame_tokens, width), 0)
    lane = lax.broadcasted_iota(jnp.int32, (frame_tokens, width), 1)
    slot = jnp.where(row < tokens, row + tile * tokens, row - tile * tokens)
    zero = jnp.zeros((frame_tokens, width), BF16)
    heads = [lane < IDM_DIM, lane >= IDM_DIM]
    for frame in range(frames):
        live = slot < counts_ref[frame]
        for pair in range(columns // width):
            lanes = slice(pair * width, (pair + 1) * width)
            rows = normed[frame * frame_tokens : (frame + 1) * frame_tokens, lanes]
            asked = jnp.concatenate([jnp.where(head, rows, zero) for head in heads], axis=0)
            weights = jnp.exp2(dot_t(asked, rows) * factor).astype(BF16)
            answers = jnp.concatenate(
                [
                    jnp.concatenate(
                        [
                            jnp.where(head & live, rows, zero),
                            jnp.where(head & live, 1.0, 0.0).astype(BF16),
                        ],
                        axis=1,
                    )
                    for head in heads
                ],
                axis=0,
            )
            both = dot(
                jnp.concatenate([weights[:frame_tokens], weights[frame_tokens:]], axis=1), answers
            )
            blended = (both[:, :width] / both[:, width:]).astype(BF16)
            store(frame, lanes, blended)


def idm_first_kernel(steps, counts_ref, own_ref, other_ref, gain_ref, *rest):
    weight_refs, out_ref = rest[:-1], rest[-1]
    tokens = own_ref.shape[1]
    tile = lax.axis_index("tile")

    def store(frame, lanes, blended):
        for which, start in ((0, tile * tokens), (1, (1 - tile) * tokens)):
            place = pl.ds(pl.multiple_of(start, tokens), tokens)
            out_ref[frame, place, lanes] = blended[which * tokens : (which + 1) * tokens]

    half = lax.axis_index("clip")
    idm_rows(tile, half, steps, counts_ref, own_ref, other_ref, gain_ref, weight_refs, store)


def idm_second_kernel(steps, counts_ref, own_ref, other_ref, gain_ref, first_ref, *rest):
    weight_refs, (out_ref, held_ref, sems) = rest[:-3], rest[-3:]
    frames, tokens = own_ref.shape[:2]
    columns = first_ref.shape[2]
    tile = lax.axis_index("tile")
    half = lax.axis_index("clip")
    wide = lambda which: pl.ds(pl.multiple_of(which * columns, columns), columns)
    copies = [pltpu.make_async_copy(first_ref, out_ref.at[:, :, wide(half)], sems.at[frames])]
    copies[0].start()
    done = [0] * frames

    def store(frame, lanes, blended):
        for which, start in ((0, tile * tokens), (1, (1 - tile) * tokens)):
            place = pl.ds(pl.multiple_of(start, tokens), tokens)
            held_ref[frame, place, lanes] = blended[which * tokens : (which + 1) * tokens]
        done[frame] += blended.shape[1]
        if done[frame] == columns:
            copy = pltpu.make_async_copy(
                held_ref.at[frame], out_ref.at[frame, :, wide(1 - half)], sems.at[frame]
            )
            copy.start()
            copies.append(copy)

    idm_rows(tile, 1 - half, steps, counts_ref, own_ref, other_ref, gain_ref, weight_refs, store)
    for copy in copies:
        copy.wait()


def idm_half(counts, steps, own, other, gain, weights, first):
    frames, tokens, width = own.shape
    columns = gain.shape[1] // 2
    flops = 4 * frames * tokens * width * columns
    operands = [own, other, gain] + ([] if first is None else [first]) + weights
    if first is None:
        kernel, out_spec, scratch = idm_first_kernel, VMEM_SPEC, []
        shape = (frames, 2 * tokens, columns)
    else:
        kernel, out_spec = idm_second_kernel, HBM_SPEC
        shape = (frames, 2 * tokens, 2 * columns)
        scratch = [pltpu.VMEM(first.shape, BF16), pltpu.SemaphoreType.DMA((frames + 1,))]
    return pl.pallas_call(
        functools.partial(kernel, steps),
        in_specs=[SMEM_SPEC] + [VMEM_SPEC] * len(operands),
        out_specs=out_spec,
        out_shape=jax.ShapeDtypeStruct(shape, BF16),
        scratch_shapes=scratch,
        name="idm_first" if first is None else "idm_second",
        compiler_params=params(16),
        cost_estimate=pl.CostEstimate(flops=flops, bytes_accessed=4 << 20, transcendentals=0),
    )(counts, *operands)


def planned(queries, keyvals, proj_weight, norm_gain, frame_counts):
    first, second, mine = prepare(frame_counts, keyvals, proj_weight, True)
    far_3 = swapped(mine, "tm", 6)
    near = swapped(mine, "tm", 2)
    beside = swapped(mine, "tm", 1)
    lead_3 = passed_along(second, "tm", 2)
    lead_2 = passed_along(first, "tm", 1)
    near_side = swapped(near, "tm", 1)
    across_1 = swapped(jnp.concatenate([near, beside], axis=0), "clip", 1)
    far_2 = swapped(far_3, "tm", 2)
    side = lax.axis_index("tm") % 2
    lead_1 = swapped(jnp.where(side == 1, lead_3, second), "tm", 1)
    far = jnp.concatenate([far_3, far_2], axis=0)
    far_side = swapped(far, "tm", 1)
    far_near = jnp.concatenate([far, near_side], axis=0)
    across_2 = swapped(far_near, "clip", 1)
    across_3 = swapped(far_side, "clip", 1)
    leads = [lead_3, lead_2, lead_1]
    own = window_attention(frame_counts, queries, keyvals, leads)
    other = swapped(own, "tile", 1)
    gain = norm_gain.reshape(1, -1)
    out = idm_half(
        frame_counts, (0, 2, 1, 6, 4, 3, 7, 5), own, other, gain,
        [mine, near, beside, far_near, far_side], None,
    )
    return idm_half(
        frame_counts, (2, 1, 6, 4, 3, 7, 5, 0), own, other, gain,
        [across_1, across_2, across_3, proj_weight], out,
    )


def general(queries, keyvals, proj_weight, norm_gain, frame_counts):
    frames_here, tile_tokens = queries.shape[:2]
    columns = proj_weight.shape[1]
    pieces = prepare(frame_counts, keyvals, proj_weight, False)
    leads = []
    for back in range(WINDOW - 1, 0, -1):
        hops = -(-back // frames_here)
        leads.append(passed_along(pieces[hops * frames_here - back], "tm", hops))
    own = window_attention(frame_counts, queries, keyvals, leads)
    weight = lax.all_gather(proj_weight, "tm", axis=0, tiled=True)
    both = lax.all_gather(own, "tile", axis=1, tiled=True)
    summed = jnp.dot(
        both.reshape(-1, both.shape[2]), weight, preferred_element_type=F32
    )
    latent = summed.astype(BF16).reshape(frames_here, 2 * tile_tokens, columns)
    normed = normalize_heads(latent, norm_gain)
    return partner_attention(normed, frame_counts)


def normalize_heads(latent_block, gain):
    width = latent_block.shape[-1]
    heads = width // IDM_DIM
    values = latent_block.astype(F32).reshape(latent_block.shape[:-1] + (heads, IDM_DIM))
    scaled = values * lax.rsqrt(jnp.mean(values * values, axis=-1, keepdims=True) + 1e-06)
    scaled = scaled * gain.reshape(heads, IDM_DIM)
    return scaled.astype(BF16).reshape(latent_block.shape)


def partner_attention(normed, frame_counts):
    frames_here, frame_tokens, width = normed.shape
    heads_here = width // IDM_DIM
    distance = PARTNER // frames_here
    before_normed, before_counts = passed_along((normed, frame_counts), "tm", distance)
    after_normed, after_counts = passed_along((normed, frame_counts), "tm", -distance)
    slot_all = jnp.arange(frame_tokens, dtype=jnp.int32)
    results = []
    for frame_index in range(frames_here):
        key_rows = jnp.concatenate(
            [before_normed[frame_index], normed[frame_index], after_normed[frame_index]], axis=0
        )
        key_rows = key_rows.reshape(3 * frame_tokens, heads_here, IDM_DIM)
        live_keys = jnp.concatenate(
            [
                slot_all < before_counts[frame_index],
                slot_all < frame_counts[frame_index],
                slot_all < after_counts[frame_index],
            ]
        )
        query_rows = normed[frame_index].reshape(frame_tokens, heads_here, IDM_DIM)
        scores = jnp.einsum(
            "ihd,jhd->ihj", query_rows, key_rows, preferred_element_type=F32
        ) * IDM_DIM ** (-0.5)
        weights = jnp.where(live_keys[None, None, :], jnp.exp(scores), 0.0)
        normalized = (weights / jnp.sum(weights, axis=-1, keepdims=True)).astype(BF16)
        blended = jnp.einsum("ihj,jhd->ihd", normalized, key_rows, preferred_element_type=F32)
        results.append(blended.astype(BF16).reshape(frame_tokens, width))
    return jnp.stack(results)


def solution(mesh):
    sizes = mesh.shape

    def local(queries, keyvals, proj_weight, norm_gain, frame_counts):
        frames_here = queries.shape[0]
        no_partner = PARTNER >= frames_here * sizes["tm"]
        eight_by_two = sizes["tm"] == 8 and sizes["clip"] == 2 and sizes["tile"] == 2
        if eight_by_two and no_partner and frames_here == 2:
            chosen = planned
        else:
            chosen = general
        return chosen(queries, keyvals, proj_weight, norm_gain, frame_counts)

    in_specs = (
        P(("clip", "tm"), "tile", None),
        P(None, ("clip", "tm"), "tile", None),
        P("tm", "tile"),
        P("tile"),
        P(("clip", "tm")),
    )
    out_specs = P(("clip", "tm"), None, "tile")
    return jax.shard_map(
        local, mesh=mesh, in_specs=in_specs, out_specs=out_specs, check_vma=False
    )
```
